32 devices in a mesh: groups: 2 (over x), tm: 16 (over z, y, core).
Axes of the slice: x: 2, y: 2, z: 4, core: 2. Of those that a mesh axis runs over, the one named last changes fastest.
Arguments:
- samples: float32 [16384, 2048], P('groups', 'tm'), parts along dimension 0, may hold values from -6 to 6
- test_matrix: float32 [4096, 256], P(('groups', 'tm')), parts along dimension 0, may hold values from -0.125 to 0.125
Outputs:
- basis: float32 [16384, 256], P(('groups', 'tm')), parts along dimension 0
- coordinates: float32 [512, 2048], P('groups', 'tm'), parts along dimension 0
The draws below stay inside these ranges and needn't reach their ends.
There are 2 independent parts, one for each index of `groups`. The reference program is written for one: setup_inputs(seed, part) draws one part's arguments, and reference() takes and returns one part's arrays. A program takes and returns all parts, laid end to end along the dimension named above; each array names one. Nothing has to cross between parts.
All inputs are finite; a program needn't handle non-finite values.
Results may differ from the reference program's by a relative error of at most 0.0003.
Values sent between devices are 32-bit elements; how exact they have to be, the bound alone decides.
No kernel may reach another device: no remote copies, remote signals or barrier semaphores. Data moves between devices by JAX's collectives and lax.ppermute only.
A program may use at most 64 MiB of HBM per device.

```python
import jax
import jax.numpy as jnp
from jax import lax

C = 8192
K = 256
S = 2048


def with_spikes(array, rng, source, target, parts, factor):
    def block_of(dim):
        return (jnp.arange(array.shape[dim]) // (array.shape[dim] // parts)).reshape((-1,) + (1,) * (array.ndim - 1 - dim))

    first = jax.random.permutation(rng, parts)[block_of(target)]
    far = (block_of(target) + parts // 2) % parts
    return jnp.where((block_of(source) == first) | (block_of(source) == far), factor * array, array)


def steps_of(key, shape, cuts, low, high):
    def one(dim, blocks):
        draws = jax.random.uniform(jax.random.fold_in(jax.random.fold_in(key, 6), dim), (blocks,), jnp.float32, low / len(cuts), high / len(cuts))
        return jnp.repeat(jnp.exp(draws), shape[dim] // blocks).reshape((-1,) + (1,) * (len(shape) - dim - 1))

    gain = one(*cuts[0])
    for cut in cuts[1:]:
        gain = gain * one(*cut)
    return gain


def centred(key, shape, width, most, cuts=(), held_as=jnp.bfloat16):
    drawn = width * jax.random.normal(key, shape, jnp.float32)
    if cuts:
        drawn = drawn * steps_of(key, shape, cuts, -0.22, 0.18)
    return jnp.clip(drawn, -most, most).astype(held_as)


def gaussian_with(key, dims, scale, bound, cuts, heavy, held_as=jnp.bfloat16):
    result = scale * jax.random.normal(key, dims, jnp.float32)
    if cuts:
        result = result * steps_of(key, dims, cuts, -0.22, 0.18)
    return jnp.clip(with_spikes(result, jax.random.fold_in(key, 3), *heavy), -bound, bound).astype(held_as)


def setup_inputs(seed: int = 0, part: int = 0) -> dict:
    keys = jax.random.split(jax.random.key(seed), 3)
    part_keys = jax.random.split(jax.random.fold_in(keys[2], part), 3)
    return {
        "samples": gaussian_with(part_keys[0], (C, S), 1.0, 6.0, ((1, 16),), (1, 0, 16, 2.0), jnp.float32),
        "test_matrix": centred(part_keys[1], (S, K), S ** -0.5, 0.125, ((0, 16),), jnp.float32),
    }


def reference(samples, test_matrix):
    highest = lax.Precision.HIGHEST
    sketch = jnp.dot(samples.astype(jnp.float32), test_matrix.astype(jnp.float32), precision=highest, preferred_element_type=jnp.float32)
    orthonormal, upper = jnp.linalg.qr(sketch)
    signs = jnp.where(jnp.diagonal(upper) < 0, -1.0, 1.0).astype(orthonormal.dtype)
    orthonormal = orthonormal * signs[None, :]
    coordinates = jnp.dot(orthonormal.T.astype(jnp.float32), samples.astype(jnp.float32), precision=highest, preferred_element_type=jnp.float32)
    basis = orthonormal * float(C) ** 0.5
    return (basis, coordinates)
```

```python
import math

import jax
import jax.numpy as jnp
from jax import lax
from jax.experimental import pallas as pl
from jax.experimental.pallas import tpu as pltpu
from jax.sharding import PartitionSpec as P

HIGHEST = lax.Precision.HIGHEST
VMEM = pl.BlockSpec(memory_space=pltpu.VMEM)
SMEM = pl.BlockSpec(memory_space=pltpu.SMEM)
SIDE = 64


def contract(a, b, dims):
    return lax.dot_general(
        a, b, (dims, ((), ())), precision=HIGHEST, preferred_element_type=jnp.float32
    )


def dot(a, b):
    return contract(a, b, ((1,), (0,)))


def split(v):
    high = v.astype(jnp.bfloat16)
    return high, (v - high.astype(jnp.float32)).astype(jnp.bfloat16)


def split_dot(a, b, dims=((1,), (0,))):
    (ah, al), (bh, bl) = split(a), split(b)

    def one(x, y):
        return lax.dot_general(x, y, (dims, ((), ())), preferred_element_type=jnp.float32)

    return one(ah, bh) + (one(ah, bl) + one(al, bh))


def factor_block(x, off):
    count = len(x)
    sub = lax.broadcasted_iota(jnp.int32, (8, 128), 0)

    def spread(v):
        return jnp.broadcast_to(v, (8, 128))

    for p in range(count):
        base = off + 8 * p
        cols = [[spread(x[t][:, base + j : base + j + 1]) for j in range(8)] for t in range(p, count)]
        d = [[spread(cols[0][j][i : i + 1, :]) for j in range(i + 1)] for i in range(8)]
        scale = []
        for j in range(8):
            scale.append(lax.rsqrt(d[j][j]))
            for i in range(j + 1, 8):
                d[i][j] = d[i][j] * scale[j]
            for i in range(j + 1, 8):
                for k in range(j + 1, i + 1):
                    d[i][k] = d[i][k] - d[i][j] * d[k][j]
        rows = []
        for j in range(8):
            r = spread(x[p][j : j + 1, :])
            for k in range(j):
                r = r - d[j][k] * rows[k]
            rows.append(r * scale[j])
        out = rows[0]
        for j in range(1, 8):
            out = jnp.where(sub == j, rows[j], out)
        x[p] = out
        for t in range(p + 1, count):
            done = []
            acc = x[t]
            for j in range(8):
                v = cols[t - p][j]
                for k in range(j):
                    v = v - d[j][k] * done[k]
                v = v * scale[j]
                done.append(v)
                acc = acc - v * rows[j]
            x[t] = acc
    return x


def eliminate(work, inv, j):
    rank = work.shape[0]
    lane = lax.broadcasted_iota(jnp.int32, (8, 128), 1)
    sub = lax.broadcasted_iota(jnp.int32, (8, 128), 0)
    start, stop = j * SIDE, (j + 1) * SIDE
    off = start % 128
    other = SIDE - off
    lanes = start // 128 * 128
    inside = (lane >= off) & (lane < off + SIDE)
    tiles = []
    for t in range(SIDE // 8):
        v = work[start + 8 * t : start + 8 * t + 8, lanes : lanes + 128]
        tiles.append(jnp.where(inside, v, jnp.where(lane - other == sub + 8 * t, 1.0, 0.0)))
    tile = jnp.concatenate(factor_block(tiles, off), 0)
    lane_of = lax.broadcasted_iota(jnp.int32, (SIDE, 128), 1)
    tile = jnp.where((lane_of >= other) & (lane_of < other + SIDE), tile, 0.0)
    rows = jnp.concatenate([work[start:stop, :], inv[start:stop, :]], 1)
    zero = jnp.zeros_like(rows)
    rows = jnp.concatenate([rows, zero] if other == 0 else [zero, rows], 0)
    panel = dot(tile, rows)
    inv[start:stop, :] = panel[:, rank:]
    if stop < rank:
        low = stop // 128 * 128
        left = panel[:, low:rank]
        column = lax.broadcasted_iota(jnp.int32, left.shape, 1) + low
        left = jnp.where(column >= stop, left, 0.0)
        update = contract(left, panel, ((0,), (0,)))
        work[low:, :] = work[low:, :] - update[:, :rank]
        inv[low:, :] = inv[low:, :] - update[:, rank:]


def call(kernel, out_shapes, args, scratch=(), flops=0, grant=12, alias=None):
    shapes = [jax.ShapeDtypeStruct(s, jnp.float32) for s in out_shapes]
    moved = 4 * sum(math.prod(a.shape) for a in (*args, *shapes))
    return pl.pallas_call(
        kernel,
        out_shape=shapes,
        in_specs=[SMEM if a.dtype == jnp.int32 else VMEM for a in args],
        out_specs=[VMEM] * len(shapes),
        scratch_shapes=[pltpu.VMEM(s, jnp.float32) for s in scratch],
        cost_estimate=pl.CostEstimate(flops=flops, bytes_accessed=moved, transcendentals=0),
        input_output_aliases=alias or {},
        compiler_params=pltpu.CompilerParams(vmem_limit_bytes=grant << 20),
    )(*args)


def blocks_of(samples, which, block, me):
    count = len(which)

    def kernel(me_ref, source, *refs):
        outs, done = refs[:count], refs[count]
        copies = []
        for k, (bits, out) in enumerate(zip(which, outs)):
            at = pl.multiple_of((me_ref[0] ^ bits) * block, block)
            copies.append(pltpu.make_async_copy(source.at[pl.ds(at, block), :], out, done.at[k]))
        for c in copies:
            c.start()
        for c in copies:
            c.wait()

    shape = jax.ShapeDtypeStruct((block, samples.shape[1]), jnp.float32)
    return pl.pallas_call(
        kernel,
        out_shape=[shape] * count,
        in_specs=[SMEM, pl.BlockSpec(memory_space=pltpu.HBM)],
        out_specs=[VMEM] * count,
        scratch_shapes=[pltpu.SemaphoreType.DMA((count,))],
        cost_estimate=pl.CostEstimate(
            flops=0, bytes_accessed=8 * count * math.prod(shape.shape), transcendentals=0
        ),
        compiler_params=pltpu.CompilerParams(vmem_limit_bytes=12 << 20),
        name="blocks",
    )(me, samples)


def sketch_of(parts, mixers, half, extra, last=False):
    count, blend = len(parts), len(mixers)
    rows, rank = parts[0].shape[0] // 2, mixers[0].shape[1]

    def kernel(*refs):
        ins = refs[: count + blend + len(extra)]
        at = slice(half * rows, (half + 1) * rows)
        left = jnp.concatenate([r[at, :] for r in ins[:count]], 1)
        mixer = jnp.concatenate([r[...] for r in ins[count : count + blend]], 0)
        total = split_dot(left, mixer)
        for r in ins[count + blend :]:
            total = total + r[...]
        refs[len(ins)][...] = total
        if last:
            refs[-1][...] = total.T

    shapes = [(rows, rank), (rank, rows)] if last else [(rows, rank)]
    depth = count * parts[0].shape[1]
    return call(kernel, shapes, [*parts, *mixers, *extra], flops=6 * rows * rank * depth)


def gram_halves(rows, turned, me):
    rank = turned[0].shape[0]
    half = rank // 2
    count = len(rows)

    def kernel(me_ref, *refs):
        keep, send, work = refs[2 * count :]
        left = jnp.concatenate([r[...] for r in refs[count : 2 * count]], 1)
        work[...] = dot(left, jnp.concatenate([r[...] for r in refs[:count]], 0))
        low = me_ref[0] & 1
        keep[...] = work[pl.ds(pl.multiple_of(low * half, half), half), :]
        send[...] = work[pl.ds(pl.multiple_of((1 - low) * half, half), half), :]

    return call(
        kernel, [(half, rank)] * 2, [me, *rows, *turned], [(rank, rank)],
        flops=12 * rank * rank * count * rows[0].shape[0],
    )


def add_halves(a, b, me):
    half, rank = a.shape[0] // 2, a.shape[1]

    def kernel(me_ref, a_ref, b_ref, keep, send):
        mid = (me_ref[0] >> 1) & 1
        for out, which in ((keep, mid), (send, 1 - mid)):
            at = pl.ds(pl.multiple_of(which * half, half), half)
            out[...] = a_ref[at, :] + b_ref[at, :]

    return call(kernel, [(half, rank)] * 2, [me, a, b])


def add_all(arrays):
    def kernel(*refs):
        total = refs[0][...]
        for r in refs[1:-1]:
            total = total + r[...]
        refs[-1][...] = total

    return call(kernel, [arrays[0].shape], arrays)[0]


def inverse_factor(quarters, me):
    part, rank = quarters[0].shape
    square = [(rank, rank)] * 2

    def first(me_ref, *refs):
        work, inv = refs[4:]
        mid, low = (me_ref[0] >> 1) & 1, me_ref[0] & 1
        for d in range(4):
            at = ((low ^ (d & 1)) * 2 + (mid ^ (d >> 1))) * part
            work[pl.ds(pl.multiple_of(at, part), part), :] = refs[d][...]
        wide = lax.broadcasted_iota(jnp.int32, (rank, rank), 1)
        tall = lax.broadcasted_iota(jnp.int32, (rank, rank), 0)
        inv[...] = jnp.where(wide == tall, 1.0, 0.0)
        eliminate(work, inv, 0)

    def later(j):
        def kernel(work_in, inv_in, work, inv):
            eliminate(work, inv, j)

        return kernel

    state = call(first, square, [me, *quarters], flops=10**9)
    for j in range(1, rank // SIDE):
        state = call(later(j), square, state, flops=10**9, alias={0: 0, 1: 1})
    return state[1]


def basis_of(sketch_rows, inverse, root):
    count, (rows, rank) = len(sketch_rows), sketch_rows[0].shape

    def kernel(*refs):
        left = jnp.concatenate([r[...] for r in refs[:count]], 0)
        refs[-1][...] = split_dot(left, refs[count][...], ((1,), (1,))) * root

    return call(
        kernel, [(count * rows, rank)], [*sketch_rows, inverse],
        flops=6 * count * rows * rank * rank,
    )[0]


def project(turned, parts, half, previous, last=False):
    count, rank = len(parts), turned.shape[0]
    cols = parts[0].shape[1]

    depth = turned.shape[1]

    def kernel(*refs):
        at = slice(half * depth, (half + 1) * depth)
        right = jnp.concatenate([r[at, :] for r in refs[1 : 1 + count]], 1)
        total = split_dot(refs[0][...], right)
        if previous is not None:
            total = total + refs[1 + count][...]
        if not last:
            refs[-1][...] = total
            return
        piece = [total[:, d * cols : (d + 1) * cols] for d in range(count)]
        refs[-3][...] = piece[0]
        refs[-2][...] = piece[2]
        refs[-1][:, :cols] = piece[1]
        refs[-1][:, cols:] = piece[3]

    shapes = [(rank, cols), (rank, cols), (rank, 2 * cols)] if last else [(rank, count * cols)]
    extra = [] if previous is None else [previous]
    return call(
        kernel, shapes, [turned, *parts, *extra],
        flops=6 * rank * count * cols * turned.shape[1],
    )


def pair_sum(second, sent):
    cols = second.shape[1]

    def kernel(a, b, out):
        out[...] = a[...] + b[:, cols:]

    return call(kernel, [second.shape], [second, sent])[0]


def coordinates_of(inverse, first, sent, across):
    cols = first.shape[1]

    def kernel(inv, a, b, c, out):
        out[...] = split_dot(inv[...], a[...] + b[:, :cols] + c[...])

    rank = inverse.shape[0]
    return call(
        kernel, [first.shape], [inverse, first, sent, across],
        flops=6 * rank * rank * cols,
    )[0]


def make_local(size):
    quads = size // 4

    def swap(x, bit):
        return lax.ppermute(x, "tm", [(i, i ^ bit) for i in range(size)])

    def total_gram(keep, sent, me):
        keep, send = add_halves(keep, sent, me)
        part = add_all([keep, swap(send, 2)])
        if quads <= 4:
            part = add_all([part] + [swap(part, 4 * e) for e in range(1, quads)])
        else:
            bit = 4
            while bit < size:
                part = add_all([part, swap(part, bit)])
                bit *= 2
        other = swap(part, 2)
        return [part, swap(part, 1), other, swap(other, 1)]

    def local(samples, test_matrix):
        return inner(samples, test_matrix)

    def inner(samples, test_matrix):
        place = lax.axis_index("tm")
        me = place.astype(jnp.int32).reshape(1)
        channels, _ = samples.shape
        block = channels // size

        order = list(reversed(range(quads)))
        mail = {}
        sends = [[(order[0], d) for d in (2, 3, 1)], [(e, d) for e in order[1:] for d in (2, 3, 1)]]
        for wanted in sends:
            found = blocks_of(samples, [4 * e + d for e, d in wanted], block, me)
            for (e, d), x in zip(wanted, found):
                mail[e, d] = swap(x, d)
        stay = blocks_of(samples, [4 * e for e in range(quads)], block, me)

        other = swap(test_matrix, 2)
        across = swap(test_matrix, 1)
        diagonal = swap(other, 1)
        mixers = [test_matrix, across, other, diagonal]

        parts = [None] * quads
        inbox = {(e, h): [] for e in range(quads) for h in (0, 1)}
        mine, turned = [None, None], [None, None]
        for e in order:
            parts[e] = [stay[e]] + [mail[e, d] for d in (1, 2, 3)]
            for h in (0, 1):
                found = sketch_of(parts[e], mixers, h, inbox[e, h], last=e == 0)
                if e:
                    step = e & -e
                    inbox[e - step, h].append(swap(found[0], 4 * step))
                else:
                    mine[h], turned[h] = found

        keep, send = gram_halves(mine, turned, me)
        quarters = total_gram(keep, swap(send, 1), me)
        inverse = inverse_factor(quarters, me)
        basis = basis_of(mine, inverse, float(channels) ** 0.5)

        held = {(0, h): turned[h] for h in (0, 1)}
        bit = quads // 2
        while bit >= 1:
            for e, h in sorted(held):
                held[e + bit, h] = swap(held[e, h], 4 * bit)
            bit //= 2
        projected = None
        sequence = sorted(held, key=lambda k: (k[1], bin(k[0]).count("1"), -k[0]))
        for e, h in sequence:
            last = (e, h) == sequence[-1]
            projected = project(held[e, h], parts[e], h, projected, last)
            if not last:
                projected = projected[0]
        first, second, send = projected
        sent = swap(send, 1)
        second = pair_sum(second, sent)
        fold = swap(second, 2)
        return basis, coordinates_of(inverse, first, sent, fold)

    return local


def solution(mesh):
    placed = (P("groups", "tm"), P(("groups", "tm"), None))
    return jax.shard_map(
        make_local(mesh.shape["tm"]),
        mesh=mesh,
        in_specs=placed,
        out_specs=(P(("groups", "tm"), None), P("groups", "tm")),
        check_vma=False,
    )
```

```python
import math

import jax
import jax.numpy as jnp
from jax import lax
from jax.experimental import pallas as pl
from jax.experimental.pallas import tpu as pltpu
from jax.sharding import PartitionSpec as P

HIGHEST = lax.Precision.HIGHEST
VMEM = pl.BlockSpec(memory_space=pltpu.VMEM)
SMEM = pl.BlockSpec(memory_space=pltpu.SMEM)
SIDE = 64


def contract(a, b, dims):
    return lax.dot_general(
        a, b, (dims, ((), ())), precision=HIGHEST, preferred_element_type=jnp.float32
    )


def dot(a, b):
    return contract(a, b, ((1,), (0,)))


def split(v):
    high = v.astype(jnp.bfloat16)
    return high, (v - high.astype(jnp.float32)).astype(jnp.bfloat16)


def split_dot(a, b, dims=((1,), (0,))):
    (ah, al), (bh, bl) = split(a), split(b)

    def one(x, y):
        return lax.dot_general(x, y, (dims, ((), ())), preferred_element_type=jnp.float32)

    return one(ah, bh) + (one(ah, bl) + one(al, bh))


def factor_block(x, off):
    count = len(x)
    sub = lax.broadcasted_iota(jnp.int32, (8, 128), 0)

    def spread(v):
        return jnp.broadcast_to(v, (8, 128))

    for p in range(count):
        base = off + 8 * p
        cols = [[spread(x[t][:, base + j : base + j + 1]) for j in range(8)] for t in range(p, count)]
        d = [[spread(cols[0][j][i : i + 1, :]) for j in range(i + 1)] for i in range(8)]
        scale = []
        for j in range(8):
            scale.append(lax.rsqrt(d[j][j]))
            for i in range(j + 1, 8):
                d[i][j] = d[i][j] * scale[j]
            for i in range(j + 1, 8):
                for k in range(j + 1, i + 1):
                    d[i][k] = d[i][k] - d[i][j] * d[k][j]
        rows = []
        for j in range(8):
            r = spread(x[p][j : j + 1, :])
            for k in range(j):
                r = r - d[j][k] * rows[k]
            rows.append(r * scale[j])
        out = rows[0]
        for j in range(1, 8):
            out = jnp.where(sub == j, rows[j], out)
        x[p] = out
        for t in range(p + 1, count):
            done = []
            acc = x[t]
            for j in range(8):
                v = cols[t - p][j]
                for k in range(j):
                    v = v - d[j][k] * done[k]
                v = v * scale[j]
                done.append(v)
                acc = acc - v * rows[j]
            x[t] = acc
    return x


def eliminate(work, inv, j):
    rank = work.shape[0]
    lane = lax.broadcasted_iota(jnp.int32, (8, 128), 1)
    sub = lax.broadcasted_iota(jnp.int32, (8, 128), 0)
    start, stop = j * SIDE, (j + 1) * SIDE
    off = start % 128
    other = SIDE - off
    lanes = start // 128 * 128
    inside = (lane >= off) & (lane < off + SIDE)
    tiles = []
    for t in range(SIDE // 8):
        v = work[start + 8 * t : start + 8 * t + 8, lanes : lanes + 128]
        tiles.append(jnp.where(inside, v, jnp.where(lane - other == sub + 8 * t, 1.0, 0.0)))
    tile = jnp.concatenate(factor_block(tiles, off), 0)
    lane_of = lax.broadcasted_iota(jnp.int32, (SIDE, 128), 1)
    tile = jnp.where((lane_of >= other) & (lane_of < other + SIDE), tile, 0.0)
    rows = jnp.concatenate([work[start:stop, :], inv[start:stop, :]], 1)
    zero = jnp.zeros_like(rows)
    rows = jnp.concatenate([rows, zero] if other == 0 else [zero, rows], 0)
    panel = dot(tile, rows)
    inv[start:stop, :] = panel[:, rank:]
    if stop < rank:
        low = stop // 128 * 128
        left = panel[:, low:rank]
        column = lax.broadcasted_iota(jnp.int32, left.shape, 1) + low
        left = jnp.where(column >= stop, left, 0.0)
        update = contract(left, panel, ((0,), (0,)))
        work[low:, :] = work[low:, :] - update[:, :rank]
        inv[low:, :] = inv[low:, :] - update[:, rank:]


def call(kernel, out_shapes, args, scratch=(), flops=0, grant=12, alias=None):
    shapes = [jax.ShapeDtypeStruct(s, jnp.float32) for s in out_shapes]
    moved = 4 * sum(math.prod(a.shape) for a in (*args, *shapes))
    return pl.pallas_call(
        kernel,
        out_shape=shapes,
        in_specs=[SMEM if a.dtype == jnp.int32 else VMEM for a in args],
        out_specs=[VMEM] * len(shapes),
        scratch_shapes=[pltpu.VMEM(s, jnp.float32) for s in scratch],
        cost_estimate=pl.CostEstimate(flops=flops, bytes_accessed=moved, transcendentals=0),
        input_output_aliases=alias or {},
        compiler_params=pltpu.CompilerParams(vmem_limit_bytes=grant << 20),
    )(*args)


def blocks_of(samples, wanted, block, me, grant):
    count, half = len(wanted), block // 2
    rows = [block if h is None else half for _, h in wanted]

    def kernel(me_ref, source, *refs):
        outs, done = refs[:count], refs[count]
        place = me_ref[0]
        copies = []
        for k, ((even, odd), h) in enumerate(wanted):
            bits = even + (odd - even) * (place & 1)
            at = pl.multiple_of((place ^ bits) * block + (h or 0) * half, half)
            part = source.at[pl.ds(at, rows[k]), :]
            copies.append(pltpu.make_async_copy(part, outs[k], done.at[k]))
        for c in copies:
            c.start()
        for c in copies:
            c.wait()

    cols = samples.shape[1]
    return pl.pallas_call(
        kernel,
        out_shape=[jax.ShapeDtypeStruct((r, cols), jnp.float32) for r in rows],
        in_specs=[SMEM, pl.BlockSpec(memory_space=pltpu.HBM)],
        out_specs=[VMEM] * count,
        scratch_shapes=[pltpu.SemaphoreType.DMA((count,))],
        cost_estimate=pl.CostEstimate(
            flops=0, bytes_accessed=8 * sum(rows) * cols, transcendentals=0
        ),
        compiler_params=pltpu.CompilerParams(vmem_limit_bytes=grant << 20),
        name="blocks",
    )(me, samples)


def half_of(ref, half, rows):
    return ref[...] if ref.shape[0] == rows else ref[half * rows : (half + 1) * rows, :]


def sketch_of(parts, mixers, half, extra, last=False):
    count, blend = len(parts), len(mixers)
    rows, rank = parts[0].shape[0] // 2, mixers[0].shape[1]

    def kernel(*refs):
        ins = refs[: count + blend + len(extra)]
        left = jnp.concatenate([half_of(r, half, rows) for r in ins[:count]], 1)
        mixer = jnp.concatenate([r[...] for r in ins[count : count + blend]], 0)
        total = split_dot(left, mixer)
        for r in ins[count + blend :]:
            total = total + r[...]
        refs[len(ins)][...] = total
        if last:
            refs[-1][...] = total.T

    shapes = [(rows, rank), (rank, rows)] if last else [(rows, rank)]
    depth = count * parts[0].shape[1]
    return call(kernel, shapes, [*parts, *mixers, *extra], flops=6 * rows * rank * depth)


def gram_halves(rows, turned, me):
    rank = turned[0].shape[0]
    half = rank // 2
    count = len(rows)

    def kernel(me_ref, *refs):
        keep, send, work = refs[2 * count :]
        left = jnp.concatenate([r[...] for r in refs[count : 2 * count]], 1)
        work[...] = dot(left, jnp.concatenate([r[...] for r in refs[:count]], 0))
        low = me_ref[0] & 1
        keep[...] = work[pl.ds(pl.multiple_of(low * half, half), half), :]
        send[...] = work[pl.ds(pl.multiple_of((1 - low) * half, half), half), :]

    return call(
        kernel, [(half, rank)] * 2, [me, *rows, *turned], [(rank, rank)],
        flops=12 * rank * rank * count * rows[0].shape[0],
    )


def add_halves(a, b, me):
    half, rank = a.shape[0] // 2, a.shape[1]

    def kernel(me_ref, a_ref, b_ref, keep, send):
        mid = (me_ref[0] >> 1) & 1
        for out, which in ((keep, mid), (send, 1 - mid)):
            at = pl.ds(pl.multiple_of(which * half, half), half)
            out[...] = a_ref[at, :] + b_ref[at, :]

    return call(kernel, [(half, rank)] * 2, [me, a, b])


def add_all(arrays):
    def kernel(*refs):
        total = refs[0][...]
        for r in refs[1:-1]:
            total = total + r[...]
        refs[-1][...] = total

    return call(kernel, [arrays[0].shape], arrays)[0]


def inverse_factor(quarters, me):
    part, rank = quarters[0].shape
    square = [(rank, rank)] * 2

    def first(me_ref, *refs):
        work, inv = refs[4:]
        mid, low = (me_ref[0] >> 1) & 1, me_ref[0] & 1
        for d in range(4):
            at = ((low ^ (d & 1)) * 2 + (mid ^ (d >> 1))) * part
            work[pl.ds(pl.multiple_of(at, part), part), :] = refs[d][...]
        wide = lax.broadcasted_iota(jnp.int32, (rank, rank), 1)
        tall = lax.broadcasted_iota(jnp.int32, (rank, rank), 0)
        inv[...] = jnp.where(wide == tall, 1.0, 0.0)
        eliminate(work, inv, 0)

    def later(j):
        def kernel(work_in, inv_in, work, inv):
            eliminate(work, inv, j)

        return kernel

    state = call(first, square, [me, *quarters], flops=10**9)
    for j in range(1, rank // SIDE):
        state = call(later(j), square, state, flops=10**9, alias={0: 0, 1: 1})
    return state[1]


def basis_of(sketch_rows, inverse, root):
    count, (rows, rank) = len(sketch_rows), sketch_rows[0].shape

    def kernel(*refs):
        left = jnp.concatenate([r[...] for r in refs[:count]], 0)
        refs[-1][...] = split_dot(left, refs[count][...], ((1,), (1,))) * root

    return call(
        kernel, [(count * rows, rank)], [*sketch_rows, inverse],
        flops=6 * count * rows * rank * rank,
    )[0]


def project(turned, parts, half, previous, last=False):
    count, rank = len(parts), turned.shape[0]
    cols = parts[0].shape[1]

    depth = turned.shape[1]

    def kernel(*refs):
        right = jnp.concatenate([half_of(r, half, depth) for r in refs[1 : 1 + count]], 1)
        total = split_dot(refs[0][...], right)
        if previous is not None:
            total = total + refs[1 + count][...]
        if not last:
            refs[-1][...] = total
            return
        piece = [total[:, d * cols : (d + 1) * cols] for d in range(count)]
        refs[-3][...] = piece[0]
        refs[-2][...] = piece[2]
        refs[-1][:, :cols] = piece[1]
        refs[-1][:, cols:] = piece[3]

    shapes = [(rank, cols), (rank, cols), (rank, 2 * cols)] if last else [(rank, count * cols)]
    extra = [] if previous is None else [previous]
    return call(
        kernel, shapes, [turned, *parts, *extra],
        flops=6 * rank * count * cols * turned.shape[1],
    )


def pair_sum(second, sent):
    cols = second.shape[1]

    def kernel(a, b, out):
        out[...] = a[...] + b[:, cols:]

    return call(kernel, [second.shape], [second, sent])[0]


def coordinates_of(inverse, first, sent, across):
    cols = first.shape[1]

    def kernel(inv, a, b, c, out):
        out[...] = split_dot(inv[...], a[...] + b[:, :cols] + c[...])

    rank = inverse.shape[0]
    return call(
        kernel, [first.shape], [inverse, first, sent, across],
        flops=6 * rank * rank * cols,
    )[0]


HALVED = (3, 2, 1, 0)


def sends_of(e):
    if e in HALVED:
        return ((2, 0), (3, 0), (1, None), (2, 1), (3, 1))
    return ((2, None), (3, None), (1, None))


def make_local(size):
    quads = size // 4

    depth = quads.bit_length() - 1
    route = [[4 << k for k in range(depth)], [4 << k for k in reversed(range(depth))]]

    def offset(slot, core):
        return sum(route[core][k] for k in range(depth) if slot >> k & 1)

    def hop(x, k):
        return lax.ppermute(x, "tm", [(i, i ^ route[i & 1][k]) for i in range(size)])

    def swap(x, bit):
        return lax.ppermute(x, "tm", [(i, i ^ bit) for i in range(size)])

    def total_gram(keep, sent, me):
        keep, send = add_halves(keep, sent, me)
        part = add_all([keep, swap(send, 2)])
        for k in range(depth):
            part = add_all([part, swap(part, 4 << k)])
        other = swap(part, 2)
        return [part, swap(part, 1), other, swap(other, 1)]

    def local(samples, test_matrix):
        return inner(samples, test_matrix)

    def inner(samples, test_matrix):
        place = lax.axis_index("tm")
        me = place.astype(jnp.int32).reshape(1)
        channels, _ = samples.shape
        block = channels // size

        def pieces(wanted, grant):
            masks = [
                (tuple(d ^ offset(e, core ^ (d & 1)) for core in (0, 1)), h) for e, d, h in wanted
            ]
            return blocks_of(samples, masks, block, me, grant)

        order = list(reversed(range(quads)))
        mail = {}
        every = [(e, d, h) for e in order for d, h in sends_of(e)]
        for k, wanted in enumerate((every[:2], every[2:])):
            if k:
                wanted += [(e, 0, None) for e in range(quads)]
            found = pieces(wanted, 50 if k else 60)
            for (e, d, h), x in zip(wanted, found):
                mail[e, d, h] = swap(x, d) if d else x

        def part(e, d, h):
            return mail[e, d, None] if (e, d, None) in mail else mail[e, d, h]

        other = swap(test_matrix, 2)
        across = swap(test_matrix, 1)
        diagonal = swap(other, 1)
        mixers = [test_matrix, across, other, diagonal]

        parts = [
            [[part(e, d, h) for d in range(4)] for h in (0, 1)] for e in range(quads)
        ]
        inbox = {(e, h): [] for e in range(quads) for h in (0, 1)}
        mine, turned = [None, None], [None, None]
        for e in order:
            for h in (0, 1):
                found = sketch_of(parts[e][h], mixers, h, inbox[e, h], last=e == 0)
                if e:
                    step = e & -e
                    inbox[e - step, h].append(hop(found[0], step.bit_length() - 1))
                else:
                    mine[h], turned[h] = found

        keep, send = gram_halves(mine, turned, me)
        quarters = total_gram(keep, swap(send, 1), me)
        inverse = inverse_factor(quarters, me)
        basis = basis_of(mine, inverse, float(channels) ** 0.5)

        held = {(0, h): turned[h] for h in (0, 1)}
        for k in reversed(range(depth)):
            for e, h in sorted(held):
                held[e + (1 << k), h] = hop(held[e, h], k)
        projected = None
        sequence = sorted(held, key=lambda k: (bin(k[0]).count("1"), -k[0], k[1]))
        for e, h in sequence:
            last = (e, h) == sequence[-1]
            projected = project(held[e, h], parts[e][h], h, projected, last)
            if not last:
                projected = projected[0]
        first, second, send = projected
        sent = swap(send, 1)
        second = pair_sum(second, sent)
        fold = swap(second, 2)
        return basis, coordinates_of(inverse, first, sent, fold)

    return local


def solution(mesh):
    placed = (P("groups", "tm"), P(("groups", "tm"), None))
    return jax.shard_map(
        make_local(mesh.shape["tm"]),
        mesh=mesh,
        in_specs=placed,
        out_specs=(P(("groups", "tm"), None), P("groups", "tm")),
        check_vma=False,
    )
```
